32 devices in a mesh: gx: 4 (over x, core), gy: 8 (over z, y).
Axes of the slice: x: 2, y: 2, z: 4, core: 2. Of those that a mesh axis runs over, the one named last changes fastest.
Arguments:
- right_side: bfloat16 [4, 8, 8, 625, 256], P('gx', 'gy'), may hold values from -6 to 6
- inverse_blocks: bfloat16 [4, 8, 8, 625, 625], P('gx', 'gy'), may hold values from -0.2 to 0.8
- lift_matrix: bfloat16 [625, 375], replicated, may hold values from -2 to 2
- plane_order: int32 [4, 8, 8], P('gx', 'gy'), may hold values from 0 to 7, each once within a row
- face_orient: int32 [4, 8, 8, 3], P('gx', 'gy'), may hold values from 0 to 7
Outputs:
- solution: bfloat16 [4, 8, 8, 625, 256], P('gx', 'gy')
The draws below stay inside these ranges and needn't reach their ends.
Inputs may be any that keep to these rules, and one draw needn't show every extreme that they name: `plane_order`: each slab's row lists the storage slots of its 8 elements from lowest to highest z, each slot once. `face_orient`: any of the eight orientations of a square face.
All inputs are finite; a program needn't handle non-finite values.
Results may differ from the reference program's by a relative error of at most 0.025.
Values may be sent and summed in bfloat16 or wider, within the bound.
A program may use at most 64 MiB of HBM per device.

```python
import jax
import jax.numpy as jnp
import numpy as np
from jax import lax

VARS = 5
NODES = 5
BLOCK = 625
FACE = 125
PLANES = 8
COLS = 256
SLABS_X = 4
SLABS_Y = 8


def draw_inverse_blocks(key, part):
    full_shape = (SLABS_X, SLABS_Y, PLANES, BLOCK, BLOCK)
    diag_key, rest_key = jax.random.split(jax.random.fold_in(key, 17))
    diagonal = jnp.exp(jax.random.uniform(diag_key, full_shape[:-1], jnp.float32, jnp.log(0.4), jnp.log(0.62)))
    coupling = jnp.clip(jax.random.normal(rest_key, full_shape, jnp.float32), -6.0, 6.0)
    identity = jnp.eye(BLOCK, dtype=jnp.float32)
    return (diagonal[..., None] * identity + 0.2 * coupling / jnp.sqrt(BLOCK * 1.0)).astype(jnp.bfloat16)


def draw_lift_matrix(key, part):
    lift_key = jax.random.fold_in(key, 29)
    full_shape = (BLOCK, 3 * FACE)
    entries = jnp.clip(jax.random.normal(lift_key, full_shape, jnp.float32), -6.0, 6.0)
    velocity = jnp.repeat(jnp.array([0.91, 1.29, 0.82], jnp.float32), FACE)
    return (entries * velocity[None, :] / jnp.sqrt(FACE * 1.0)).astype(jnp.bfloat16)


def set_ends(drawn, rng, least, high):
    extent = drawn.shape
    index_at = [jax.random.randint(jax.random.fold_in(rng, axis), (), 0, extent[axis]) for axis in range(len(extent))]
    drawn = drawn.at[tuple(index_at)].set(least)
    longest = extent.index(max(extent))
    index_at[longest] = (index_at[longest] + 1) % extent[longest]
    return drawn.at[tuple(index_at)].set(high)


def block_scale(own_key, dims, shards, smallest, top_value):
    loudness = 1.0
    for position, parts in shards:
        draws = jax.random.uniform(jax.random.fold_in(jax.random.fold_in(own_key, 6), position), (parts,), jnp.float32, smallest / len(shards), top_value / len(shards))
        loudness = loudness * jnp.repeat(jnp.exp(draws), dims[position] // parts).reshape((-1,) + (1,) * (len(dims) - 1 - position))
    return loudness


def noise(stream_key, dims, scale, limit, pieces=(), kind=jnp.bfloat16):
    values = jax.random.normal(stream_key, dims, jnp.float32) * scale
    if len(pieces) > 0:
        values = block_scale(stream_key, dims, pieces, -0.22, 0.18) * values
    return jnp.clip(values, min=-limit, max=limit).astype(kind)


def setup_inputs(seed: int = 0) -> dict:
    streams_of = jax.random.split(jax.random.key(seed), 6)
    right_side = noise(streams_of[0], (SLABS_X, SLABS_Y, PLANES, BLOCK, COLS), 1.0, 6.0, ((0, 4), (1, 8)))
    inverse_blocks = draw_inverse_blocks(jax.random.fold_in(streams_of[5], 71), 0)
    lift_matrix = draw_lift_matrix(jax.random.fold_in(streams_of[5], 71), 0)
    plane_order = jax.vmap(lambda own: jax.random.permutation(own, PLANES))(jax.random.split(streams_of[3], SLABS_X * SLABS_Y)).reshape((SLABS_X, SLABS_Y, PLANES)).astype(jnp.int32)
    face_orient = set_ends(jax.random.randint(streams_of[4], (SLABS_X, SLABS_Y, PLANES, 3), 0, 8), jax.random.fold_in(streams_of[4], 1), 0, 7).astype(jnp.int32)
    return dict(right_side=right_side, inverse_blocks=inverse_blocks, lift_matrix=lift_matrix, plane_order=plane_order, face_orient=face_orient)


def orient_table():
    lookup_table = np.zeros((8, FACE), np.int32)
    for orient in range(8):
        for variable in range(VARS):
            for first in range(NODES):
                for second in range(NODES):
                    if orient & 1:
                        first_new, second_new = second, first
                    else:
                        first_new, second_new = first, second
                    if orient & 2:
                        first_new = NODES - 1 - first_new
                    if orient & 4:
                        second_new = NODES - 1 - second_new
                    target = variable * NODES * NODES + first * NODES + second
                    lookup_table[orient, target] = variable * NODES * NODES + first_new * NODES + second_new
    return lookup_table


def select_matrices(orients):
    lookup = jnp.asarray(orient_table())
    codes = jnp.arange(8, dtype=jnp.int32)[:, None]
    chosen = jnp.sum(jnp.where(orients[..., None, None] == codes, lookup, 0), axis=-2)
    return (chosen[..., None] == jnp.arange(FACE, dtype=jnp.int32)).astype(jnp.float32)


def face_traces(block):
    leading = block.shape[:-2]
    columns = block.shape[-1]
    shaped = block.reshape(leading + (VARS, NODES, NODES, NODES, columns))
    along_x = shaped[..., :, NODES - 1, :, :, :].reshape(leading + (FACE, columns))
    along_y = shaped[..., :, :, NODES - 1, :, :].reshape(leading + (FACE, columns))
    along_z = shaped[..., :, :, :, NODES - 1, :].reshape(leading + (FACE, columns))
    return jnp.stack([along_x, along_y, along_z], axis=-3)


def reference(right_side, inverse_blocks, lift_matrix, plane_order, face_orient):
    across = jnp.arange(SLABS_X, dtype=jnp.int32)
    solution = jnp.zeros(right_side.shape, jnp.bfloat16)
    z_traces = jnp.zeros((SLABS_X, SLABS_Y, FACE, COLS), jnp.bfloat16)
    lift_wide = lift_matrix.astype(jnp.float32)
    for plane in range(PLANES):
        slots = plane_order[:, :, plane]
        z_before = z_traces

        def diagonal(carry, sweep):
            x_traces, y_traces, next_z, solution = carry
            column = sweep - across
            is_live = (column >= 0) & (column < SLABS_Y)
            clipped = jnp.clip(column, 0, SLABS_Y - 1).astype(jnp.int32)
            left_slab = jnp.maximum(across - 1, 0).astype(jnp.int32)
            below_slab = jnp.maximum(clipped - 1, 0).astype(jnp.int32)
            from_x = jnp.where((across > 0)[:, None, None], x_traces[left_slab, clipped], 0)
            from_y = jnp.where((clipped > 0)[:, None, None], y_traces[across, below_slab], 0)
            from_z = z_before[across, clipped]
            slot_ids = slots[across, clipped]
            source_rows = right_side[across, clipped, slot_ids]
            blocks = inverse_blocks[across, clipped, slot_ids]
            orients = face_orient[across, clipped, slot_ids]
            incoming = jnp.stack([from_x, from_y, from_z], axis=1).astype(jnp.float32)
            select = select_matrices(orients)
            turned = jnp.einsum('edqc,edcn->edqn', select, incoming).astype(jnp.bfloat16)
            turned = turned.reshape(SLABS_X, 3 * FACE, COLS).astype(jnp.float32)
            source = (source_rows.astype(jnp.float32) - jnp.einsum('bq,eqn->ebn', lift_wide, turned)).astype(jnp.bfloat16)
            result = jnp.einsum('ebc,ecn->ebn', blocks.astype(jnp.float32), source.astype(jnp.float32)).astype(jnp.bfloat16)
            traces = face_traces(result)
            live_mask = is_live[:, None, None]
            x_traces = x_traces.at[across, clipped].set(jnp.where(live_mask, traces[:, 0], x_traces[across, clipped]))
            y_traces = y_traces.at[across, clipped].set(jnp.where(live_mask, traces[:, 1], y_traces[across, clipped]))
            next_z = next_z.at[across, clipped].set(jnp.where(live_mask, traces[:, 2], next_z[across, clipped]))
            solution = solution.at[across, clipped, slot_ids].set(jnp.where(live_mask, result, solution[across, clipped, slot_ids]))
            return (x_traces, y_traces, next_z, solution), None

        blank = jnp.zeros((SLABS_X, SLABS_Y, FACE, COLS), jnp.bfloat16)
        finished, unused = lax.scan(diagonal, (blank, blank, blank, solution), jnp.arange(SLABS_X + SLABS_Y - 1, dtype=jnp.int32))
        z_traces = finished[2]
        solution = finished[3]
    return solution
```

```python
import functools

import jax
import jax.numpy as jnp
import numpy as np
from jax import lax
from jax.experimental import pallas as pl
from jax.experimental.pallas import tpu as pltpu
from jax.sharding import PartitionSpec as P

VARS = 5
NODES = 5
SQUARE = NODES * NODES
FACE = VARS * SQUARE
BLOCK = FACE * NODES
LANE = 128
CHUNKS = 2
MESH = pl.DeviceIdType.MESH


def orient_table():
    table = np.zeros((8, LANE, LANE), np.float32)
    for orient in range(8):
        for variable in range(VARS):
            for first in range(NODES):
                for second in range(NODES):
                    p, q = (second, first) if orient & 1 else (first, second)
                    if orient & 2:
                        p = NODES - 1 - p
                    if orient & 4:
                        q = NODES - 1 - q
                    target = variable * SQUARE + first * NODES + second
                    table[orient, target, variable * SQUARE + p * NODES + q] = 1.0
    return table


def dot(a, b):
    return jnp.dot(a, b, preferred_element_type=jnp.float32)


def sweep_kernel(
    order, orient, table_hbm, lift_hbm, rhs_hbm, inv_hbm, sol,
    table, lift, rhs, inv, padded, turned, full_m, wide_m, part_m, full_r, trace_m, trace_r,
    inc, out, load_sem, x_send, y_send, x_recv, y_recv,
):
    planes, columns = rhs.shape[0], rhs.shape[2]
    width = columns // CHUNKS
    two, three = 2 * LANE, 3 * LANE
    count_x, count_y = lax.axis_size("gx"), lax.axis_size("gy")
    me_x, me_y = lax.axis_index("gx"), lax.axis_index("gy")
    has_left, has_right = me_x > 0, me_x < count_x - 1
    has_below, has_above = me_y > 0, me_y < count_y - 1

    loads = [
        pltpu.make_async_copy(source, target, load_sem.at[i])
        for i, (source, target) in enumerate(
            [(lift_hbm, lift), (table_hbm, table), (rhs_hbm, rhs), (inv_hbm, inv)]
        )
    ]
    for load in loads:
        load.start()

    barrier = pltpu.get_barrier_semaphore()
    for present, x, y in (
        (has_left, me_x - 1, me_y),
        (has_right, me_x + 1, me_y),
        (has_below, me_x, me_y - 1),
        (has_above, me_x, me_y + 1),
    ):
        @pl.when(present)
        def _():
            pl.semaphore_signal(barrier, inc=1, device_id=(x, y), device_id_type=MESH)

    part_m[...] = jnp.zeros_like(part_m)
    trace_r[...] = jnp.zeros_like(trace_r)
    out[0] = jnp.zeros(out.shape[1:], out.dtype)

    @pl.when(me_x == 0)
    def _():
        inc[:, :, :LANE, :] = jnp.zeros((planes, CHUNKS, LANE, width), inc.dtype)

    @pl.when(me_y == 0)
    def _():
        inc[:, :, LANE:, :] = jnp.zeros((planes, CHUNKS, LANE, width), inc.dtype)

    row = lax.broadcasted_iota(jnp.int32, (3 * FACE, three), 0)
    col = lax.broadcasted_iota(jnp.int32, (3 * FACE, three), 1)
    face = jnp.where(col >= two, 2, jnp.where(col >= LANE, 1, 0))
    inside = col - face * LANE
    spread = ((inside < FACE) & (row == face * FACE + inside)).astype(jnp.float32).astype(jnp.bfloat16)
    loads[0].wait()
    padded[...] = dot(lift[...], spread).astype(jnp.bfloat16)
    for load in loads[1:]:
        load.wait()

    def pick(source, put):
        for v in range(VARS):
            put(v * SQUARE, source[pl.ds(v * FACE + FACE - SQUARE, SQUARE), :])
        for v in range(VARS * NODES):
            put(LANE + v * NODES, source[pl.ds(v * SQUARE + SQUARE - NODES, NODES), :])
        put(two, source[pl.ds(NODES - 1, FACE, stride=NODES), :])

    def prepare(k):
        slot = order[k]
        for d in range(3):
            tile = slice(d * LANE, (d + 1) * LANE)
            turned[:, tile] = dot(padded[:, tile], table[orient[slot * 3 + d]]).astype(jnp.bfloat16)
        block = inv[slot]
        moved = dot(block, turned[...])
        full_m[k] = moved.astype(jnp.bfloat16)
        for j in range(3):
            wide_m[j] = moved[:, j * LANE : (j + 1) * LANE]
        plain = dot(block, rhs[slot])
        for j in range(columns // LANE):
            full_r[k, j] = plain[:, j * LANE : (j + 1) * LANE]
        for j in range(3):
            def put_m(start, rows):
                part_m[j, pl.ds(start, rows.shape[0]), :] = rows
            pick(wide_m.at[j], put_m)
            trace_m[k, :, j * LANE : (j + 1) * LANE] = part_m[j].astype(jnp.bfloat16)
        for j in range(columns // LANE):
            def put_r(start, rows):
                trace_r[k, j, pl.ds(start, rows.shape[0]), :] = rows
            pick(full_r.at[k, j], put_r)

    def base_of(ref, k, c):
        per = width // LANE
        return jnp.concatenate([ref[k, c * per + j] for j in range(per)], axis=-1)

    def hop(k, c, axis):
        rows = pl.ds(axis * LANE, LANE)
        send, recv = ((x_send, x_recv), (y_send, y_recv))[axis]
        return pltpu.make_async_remote_copy(
            src_ref=out.at[k + 1, c, rows, :],
            dst_ref=inc.at[k, c, rows, :],
            send_sem=send.at[k, c],
            recv_sem=recv.at[k, c],
            device_id=((me_x + 1, me_y), (me_x, me_y + 1))[axis],
            device_id_type=MESH,
        )

    def advance(k, c):
        started = base_of(trace_r, k, c) - dot(trace_m[k, :, two:], out[k, c, two:, :])

        @pl.when(has_left)
        def _():
            hop(k, c, 0).wait_recv()

        @pl.when(has_below)
        def _():
            hop(k, c, 1).wait_recv()

        arrived = inc[k, c]
        out[k + 1, c, :two, :] = (started[:two] - dot(trace_m[k, :two, :two], arrived)).astype(jnp.bfloat16)

        @pl.when(has_above)
        def _():
            hop(k, c, 1).start()

        @pl.when(has_right)
        def _():
            hop(k, c, 0).start()

        out[k + 1, c, two:, :] = (started[two:] - dot(trace_m[k, two:, :two], arrived)).astype(jnp.bfloat16)

    def finish(k, c):
        lifted = dot(full_m[k, :, :two], inc[k, c]) + dot(full_m[k, :, two:], out[k, c, two:, :])
        sol[k, :, c * width : (c + 1) * width] = (base_of(full_r, k, c) - lifted).astype(jnp.bfloat16)

    lead = jnp.minimum(1 + 2 * (me_x + me_y), planes)

    def ahead(k, carry):
        prepare(k)
        return carry

    lax.fori_loop(0, lead, ahead, 0)

    neighbours = sum(p.astype(jnp.int32) for p in (has_left, has_right, has_below, has_above))
    pl.semaphore_wait(barrier, neighbours)

    def step(k, carry):
        for c in range(CHUNKS):
            advance(k, c)

        @pl.when(k + lead < planes)
        def _():
            prepare(k + lead)

        for c in range(CHUNKS):
            finish(k, c)
        return carry

    lax.fori_loop(0, planes, step, 0)

    def drain(k, carry):
        for c in range(CHUNKS):
            @pl.when(has_right)
            def _():
                hop(k, c, 0).wait_send()

            @pl.when(has_above)
            def _():
                hop(k, c, 1).wait_send()
        return carry

    lax.fori_loop(0, planes, drain, 0)


def place_kernel(order, sol, out, sems):
    planes = sol.shape[0]
    copies = [pltpu.make_async_copy(sol.at[k], out.at[order[k]], sems.at[k]) for k in range(planes)]
    for copy in copies:
        copy.start()
    for copy in copies:
        copy.wait()


def on_device(right_side, inverse_blocks, lift_matrix, plane_order, face_orient):
    rhs, inv = right_side[0, 0], inverse_blocks[0, 0]
    order = plane_order[0, 0]
    orient = face_orient[0, 0].reshape(-1)
    planes, block, columns = rhs.shape
    tiles = columns // LANE
    width = columns // CHUNKS
    two, three = 2 * LANE, 3 * LANE
    bf16, f32 = jnp.bfloat16, jnp.float32
    table = jnp.asarray(orient_table(), bf16)
    smem = pl.BlockSpec(memory_space=pltpu.SMEM)
    vmem = pl.BlockSpec(memory_space=pltpu.VMEM)
    anywhere = pl.BlockSpec(memory_space=pl.ANY)
    sol = pl.pallas_call(
        sweep_kernel,
        out_shape=jax.ShapeDtypeStruct(rhs.shape, bf16),
        in_specs=[smem, smem] + [anywhere] * 4,
        out_specs=vmem,
        scratch_shapes=[
            pltpu.VMEM(table.shape, bf16),
            pltpu.VMEM(lift_matrix.shape, bf16),
            pltpu.VMEM(rhs.shape, bf16),
            pltpu.VMEM(inv.shape, bf16),
            pltpu.VMEM((block, three), bf16),
            pltpu.VMEM((block, three), bf16),
            pltpu.VMEM((planes, block, three), bf16),
            pltpu.VMEM((3, block, LANE), f32),
            pltpu.VMEM((3, three, LANE), f32),
            pltpu.VMEM((planes, tiles, block, LANE), f32),
            pltpu.VMEM((planes, three, three), bf16),
            pltpu.VMEM((planes, tiles, three, LANE), f32),
            pltpu.VMEM((planes, CHUNKS, two, width), bf16),
            pltpu.VMEM((planes + 1, CHUNKS, three, width), bf16),
            pltpu.SemaphoreType.DMA((4,)),
            pltpu.SemaphoreType.DMA((planes, CHUNKS)),
            pltpu.SemaphoreType.DMA((planes, CHUNKS)),
            pltpu.SemaphoreType.DMA((planes, CHUNKS)),
            pltpu.SemaphoreType.DMA((planes, CHUNKS)),
        ],
        compiler_params=pltpu.CompilerParams(
            collective_id=0, has_side_effects=True, vmem_limit_bytes=56 * 1024 * 1024
        ),
    )(order, orient, table, lift_matrix, rhs, inv)
    result = pl.pallas_call(
        place_kernel,
        out_shape=jax.ShapeDtypeStruct(rhs.shape, bf16),
        in_specs=[smem, vmem],
        out_specs=anywhere,
        scratch_shapes=[pltpu.SemaphoreType.DMA((planes,))],
    )(order, sol)
    return result[None, None]


def solution(mesh):
    placed = (
        P("gx", "gy", None, None, None),
        P("gx", "gy", None, None, None),
        P(),
        P("gx", "gy", None),
        P("gx", "gy", None, None),
    )
    return jax.shard_map(
        on_device,
        mesh=mesh,
        in_specs=placed,
        out_specs=P("gx", "gy", None, None, None),
        check_vma=False,
    )
```

```python
import functools

import jax
import jax.numpy as jnp
import numpy as np
from jax import lax
from jax.experimental import pallas as pl
from jax.experimental.pallas import tpu as pltpu
from jax.sharding import PartitionSpec as P

VARS = 5
NODES = 5
SQUARE = NODES * NODES
FACE = VARS * SQUARE
BLOCK = FACE * NODES
LANE = 128
CHUNKS = 2
MESH = pl.DeviceIdType.MESH


def orient_table():
    table = np.zeros((8, LANE, LANE), np.float32)
    for orient in range(8):
        for variable in range(VARS):
            for first in range(NODES):
                for second in range(NODES):
                    p, q = (second, first) if orient & 1 else (first, second)
                    if orient & 2:
                        p = NODES - 1 - p
                    if orient & 4:
                        q = NODES - 1 - q
                    target = variable * SQUARE + first * NODES + second
                    table[orient, target, variable * SQUARE + p * NODES + q] = 1.0
    return table


def dot(a, b):
    return jnp.dot(a, b, preferred_element_type=jnp.float32)


def row_chunks(block):
    return [(start, min(LANE, block - start)) for start in range(0, block, LANE)]


def sweep_kernel(
    order, orient, table_hbm, lift_hbm, rhs_hbm, inv_hbm, sol,
    table, lift, raw_r, raw_b, stage, rhs, inv, padded, turned, wide, part, picked, trace_m, trace_r,
    inc, out, load_sem, r_sem, b_sem, x_send, y_send, x_recv, y_recv,
):
    planes, block, columns = rhs.shape
    width = columns // CHUNKS
    two, three = 2 * LANE, 3 * LANE
    chunks = row_chunks(block)
    tiles = [(t, min(LANE, block - t)) for t in range(0, block, LANE)]
    count_x, count_y = lax.axis_size("gx"), lax.axis_size("gy")
    me_x, me_y = lax.axis_index("gx"), lax.axis_index("gy")
    has_left, has_right = me_x > 0, me_x < count_x - 1
    has_below, has_above = me_y > 0, me_y < count_y - 1

    loads = [
        pltpu.make_async_copy(source, target, load_sem.at[i])
        for i, (source, target) in enumerate([(lift_hbm, lift), (table_hbm, table)])
    ]
    for load in loads:
        load.start()

    def fetch(i, start, size):
        rows = pl.ds(start, size)
        return (
            pltpu.make_async_copy(rhs_hbm.at[rows], raw_r.at[rows], r_sem.at[i]),
            pltpu.make_async_copy(inv_hbm.at[rows], raw_b.at[rows], b_sem.at[i]),
        )

    for i, (start, size) in enumerate(chunks):
        for copy in fetch(i, start, size):
            copy.start()

    barrier = pltpu.get_barrier_semaphore()
    for present, x, y in (
        (has_left, me_x - 1, me_y),
        (has_right, me_x + 1, me_y),
        (has_below, me_x, me_y - 1),
        (has_above, me_x, me_y + 1),
    ):
        @pl.when(present)
        def _():
            pl.semaphore_signal(barrier, inc=1, device_id=(x, y), device_id_type=MESH)

    part[...] = jnp.zeros_like(part)
    out[0] = jnp.zeros(out.shape[1:], out.dtype)

    @pl.when(me_x == 0)
    def _():
        inc[:, :, :LANE, :] = jnp.zeros((planes, CHUNKS, LANE, width), inc.dtype)

    @pl.when(me_y == 0)
    def _():
        inc[:, :, LANE:, :] = jnp.zeros((planes, CHUNKS, LANE, width), inc.dtype)

    row = lax.broadcasted_iota(jnp.int32, (3 * FACE, three), 0)
    col = lax.broadcasted_iota(jnp.int32, (3 * FACE, three), 1)
    face = jnp.where(col >= two, 2, jnp.where(col >= LANE, 1, 0))
    inside = col - face * LANE
    spread = ((inside < FACE) & (row == face * FACE + inside)).astype(jnp.float32).astype(jnp.bfloat16)
    loads[0].wait()
    padded[...] = lax.dot_general(
        lift[...], spread, (((0,), (0,)), ((), ())), preferred_element_type=jnp.float32
    ).astype(jnp.bfloat16)
    loads[1].wait()

    def split(raw, into, rows, size, lanes, t):
        mixed = raw[rows, :, lanes].astype(jnp.float32)
        wide_lanes = mixed.shape[-1]
        stage[t, : size * planes, :wide_lanes] = mixed.reshape(size * planes, wide_lanes)
        for s in range(planes):
            apart = stage[t, pl.ds(s, size, stride=planes), :]
            into[s, rows, lanes] = apart[:, :wide_lanes].astype(jnp.bfloat16)

    def arrange(i, start, size):
        for copy in fetch(i, start, size):
            copy.wait()
        rows = pl.ds(start, size)
        for t, (first, wide_lanes) in enumerate(tiles):
            split(raw_b, inv, rows, size, slice(first, first + wide_lanes), t)
        for t in range(columns // LANE):
            split(raw_r, rhs, rows, size, slice(t * LANE, (t + 1) * LANE), len(tiles) + t)

    def arrange_full(i, carry):
        arrange(i, pl.multiple_of(i * LANE, LANE), LANE)
        return carry

    whole = block // LANE
    lax.fori_loop(0, whole, arrange_full, 0)
    for i, (start, size) in list(enumerate(chunks))[whole:]:
        arrange(i, start, size)

    def pick(source, put):
        for v in range(VARS):
            put(v * SQUARE, source[pl.ds(v * FACE + FACE - SQUARE, SQUARE), :])
        for v in range(VARS * NODES):
            put(LANE + v * NODES, source[pl.ds(v * SQUARE + SQUARE - NODES, NODES), :])
        put(two, source[pl.ds(NODES - 1, FACE, stride=NODES), :])

    def prepare(k):
        slot = order[k]
        for d in range(3):
            tile = slice(d * LANE, (d + 1) * LANE)
            turned[k, :, tile] = dot(padded[:, tile], table[orient[d, 0, slot]]).astype(jnp.bfloat16)
        for t, (first, wide_lanes) in enumerate(tiles):
            wide[t, :, :wide_lanes] = inv[slot, :, first : first + wide_lanes].astype(jnp.float32)

            def put(start, rows):
                part[t, pl.ds(start, rows.shape[0]), :] = rows

            pick(wide.at[t], put)
            picked[:, first : first + wide_lanes] = part[t, :, :wide_lanes].astype(jnp.bfloat16)
        trace_m[k] = dot(picked[...], turned[k]).astype(jnp.bfloat16)
        plain = dot(picked[...], rhs[slot])
        for c in range(CHUNKS):
            trace_r[k, c] = plain[:, c * width : (c + 1) * width]

    def hop(k, c, axis):
        rows = pl.ds(axis * LANE, LANE)
        send, recv = ((x_send, x_recv), (y_send, y_recv))[axis]
        return pltpu.make_async_remote_copy(
            src_ref=out.at[k + 1, c, rows, :],
            dst_ref=inc.at[k, c, rows, :],
            send_sem=send.at[k, c],
            recv_sem=recv.at[k, c],
            device_id=((me_x + 1, me_y), (me_x, me_y + 1))[axis],
            device_id_type=MESH,
        )

    def advance(k, c):
        started = trace_r[k, c] - dot(trace_m[k, :, two:], out[k, c, two:, :])

        @pl.when(has_left)
        def _():
            hop(k, c, 0).wait_recv()

        @pl.when(has_below)
        def _():
            hop(k, c, 1).wait_recv()

        arrived = inc[k, c]
        out[k + 1, c, :two, :] = (started[:two] - dot(trace_m[k, :two, :two], arrived)).astype(jnp.bfloat16)

        @pl.when(has_above)
        def _():
            hop(k, c, 1).start()

        @pl.when(has_right)
        def _():
            hop(k, c, 0).start()

        out[k + 1, c, two:, :] = (started[two:] - dot(trace_m[k, two:, :two], arrived)).astype(jnp.bfloat16)

    def finish(k):
        slot = order[k]
        behind = jnp.concatenate([inc[k, c] for c in range(CHUNKS)], axis=-1)
        under = jnp.concatenate([out[k, c, two:, :] for c in range(CHUNKS)], axis=-1)
        lifted = dot(turned[k, :, :two], behind) + dot(turned[k, :, two:], under)
        source = (rhs[slot].astype(jnp.float32) - lifted).astype(jnp.bfloat16)
        sol[k] = dot(inv[slot], source).astype(jnp.bfloat16)

    distance = me_x + me_y
    lead = jnp.minimum(1 + 2 * distance, planes)
    near = distance * 2 <= count_x + count_y - 2

    def ahead(k, carry):
        prepare(k)
        return carry

    lax.fori_loop(0, lead, ahead, 0)

    neighbours = sum(p.astype(jnp.int32) for p in (has_left, has_right, has_below, has_above))
    pl.semaphore_wait(barrier, neighbours)

    def step(k, carry):
        for c in range(CHUNKS):
            advance(k, c)

        @pl.when(k + lead < planes)
        def _():
            prepare(k + lead)

        @pl.when(jnp.logical_not(near))
        def _():
            finish(k)

        return carry

    lax.fori_loop(0, planes, step, 0)

    @pl.when(near)
    def _():
        def late(k, carry):
            finish(k)
            return carry

        lax.fori_loop(0, planes, late, 0)

    def drain(k, carry):
        for c in range(CHUNKS):
            @pl.when(has_right)
            def _():
                hop(k, c, 0).wait_send()

            @pl.when(has_above)
            def _():
                hop(k, c, 1).wait_send()
        return carry

    lax.fori_loop(0, planes, drain, 0)


def place_kernel(order, sol, out, stage):
    planes, rows, columns = sol.shape
    for t in range(columns // LANE):
        lanes = slice(t * LANE, (t + 1) * LANE)
        for k in range(planes):
            stage[t, pl.ds(order[k], rows, stride=planes), :] = sol[k, :, lanes].astype(jnp.float32)
        out[:, :, lanes] = stage[t].reshape(rows, planes, LANE).astype(jnp.bfloat16)


def on_device(right_side, inverse_blocks, lift_matrix, plane_order, face_orient):
    rhs = jnp.transpose(right_side, (0, 1, 3, 2, 4))[0, 0]
    inv = jnp.transpose(inverse_blocks, (0, 1, 3, 2, 4))[0, 0]
    order = plane_order[0, 0]
    orient = jnp.transpose(face_orient, (0, 3, 1, 2))[0]
    block, planes, columns = rhs.shape
    tiles = pl.cdiv(block, LANE)
    chunks = len(row_chunks(block))
    width = columns // CHUNKS
    two, three = 2 * LANE, 3 * LANE
    bf16, f32 = jnp.bfloat16, jnp.float32
    table = jnp.asarray(orient_table(), bf16)
    lift = lift_matrix.T
    smem = pl.BlockSpec(memory_space=pltpu.SMEM)
    vmem = pl.BlockSpec(memory_space=pltpu.VMEM)
    anywhere = pl.BlockSpec(memory_space=pl.ANY)
    sol = pl.pallas_call(
        sweep_kernel,
        out_shape=jax.ShapeDtypeStruct((planes, block, columns), bf16),
        in_specs=[smem, smem] + [anywhere] * 4,
        out_specs=vmem,
        scratch_shapes=[
            pltpu.VMEM(table.shape, bf16),
            pltpu.VMEM(lift.shape, bf16),
            pltpu.VMEM(rhs.shape, bf16),
            pltpu.VMEM(inv.shape, bf16),
            pltpu.VMEM((tiles + columns // LANE, LANE * planes, LANE), f32),
            pltpu.VMEM((planes, block, columns), bf16),
            pltpu.VMEM((planes, block, block), bf16),
            pltpu.VMEM((block, three), bf16),
            pltpu.VMEM((planes, block, three), bf16),
            pltpu.VMEM((tiles, block, LANE), f32),
            pltpu.VMEM((tiles, three, LANE), f32),
            pltpu.VMEM((three, block), bf16),
            pltpu.VMEM((planes, three, three), bf16),
            pltpu.VMEM((planes, CHUNKS, three, width), f32),
            pltpu.VMEM((planes, CHUNKS, two, width), bf16),
            pltpu.VMEM((planes + 1, CHUNKS, three, width), bf16),
            pltpu.SemaphoreType.DMA((2,)),
            pltpu.SemaphoreType.DMA((chunks,)),
            pltpu.SemaphoreType.DMA((chunks,)),
            pltpu.SemaphoreType.DMA((planes, CHUNKS)),
            pltpu.SemaphoreType.DMA((planes, CHUNKS)),
            pltpu.SemaphoreType.DMA((planes, CHUNKS)),
            pltpu.SemaphoreType.DMA((planes, CHUNKS)),
        ],
        compiler_params=pltpu.CompilerParams(
            collective_id=0, has_side_effects=True, vmem_limit_bytes=60 * 1024 * 1024
        ),
    )(order, orient, table, lift, rhs, inv)
    result = pl.pallas_call(
        place_kernel,
        out_shape=jax.ShapeDtypeStruct(rhs.shape, bf16),
        grid_spec=pltpu.PrefetchScalarGridSpec(
            num_scalar_prefetch=1,
            grid=(chunks,),
            in_specs=[pl.BlockSpec((planes, LANE, columns), lambda i, o: (0, i, 0))],
            out_specs=pl.BlockSpec((LANE, planes, columns), lambda i, o: (i, 0, 0)),
            scratch_shapes=[pltpu.VMEM((columns // LANE, LANE * planes, LANE), f32)],
        ),
    )(order, sol)
    return jnp.transpose(result[None, None], (0, 1, 3, 2, 4))


def solution(mesh):
    placed = (
        P("gx", "gy", None, None, None),
        P("gx", "gy", None, None, None),
        P(),
        P("gx", "gy", None),
        P("gx", "gy", None, None),
    )
    return jax.shard_map(
        on_device,
        mesh=mesh,
        in_specs=placed,
        out_specs=P("gx", "gy", None, None, None),
        check_vma=False,
    )
```

```python
import functools

import jax
import jax.numpy as jnp
import numpy as np
from jax import lax
from jax.experimental import pallas as pl
from jax.experimental.pallas import tpu as pltpu
from jax.sharding import PartitionSpec as P

VARS = 5
NODES = 5
SQUARE = NODES * NODES
FACE = VARS * SQUARE
BLOCK = FACE * NODES
LANE = 128
CHUNKS = 2
MESH = pl.DeviceIdType.MESH


def orient_table():
    table = np.zeros((8, LANE, LANE), np.float32)
    for orient in range(8):
        for variable in range(VARS):
            for first in range(NODES):
                for second in range(NODES):
                    p, q = (second, first) if orient & 1 else (first, second)
                    if orient & 2:
                        p = NODES - 1 - p
                    if orient & 4:
                        q = NODES - 1 - q
                    target = variable * SQUARE + first * NODES + second
                    table[orient, target, variable * SQUARE + p * NODES + q] = 1.0
    return table


def dot(a, b):
    return jnp.dot(a, b, preferred_element_type=jnp.float32)


def row_chunks(block):
    return [(start, min(LANE, block - start)) for start in range(0, block, LANE)]


def sweep_kernel(
    order, orient, table_hbm, lift_hbm, rhs_hbm, inv_hbm, sol,
    table, lift, raw_r, raw_b, stage, rhs, inv, padded, turned, wide, part, picked, trace_m, trace_r,
    inc, out, load_sem, r_sem, b_sem, x_send, y_send, x_recv, y_recv,
):
    planes, block, columns = rhs.shape
    width = columns // CHUNKS
    two, three = 2 * LANE, 3 * LANE
    chunks = row_chunks(block)
    tiles = [(t, min(LANE, block - t)) for t in range(0, block, LANE)]
    count_x, count_y = lax.axis_size("gx"), lax.axis_size("gy")
    me_x, me_y = lax.axis_index("gx"), lax.axis_index("gy")
    has_left, has_right = me_x > 0, me_x < count_x - 1
    has_below, has_above = me_y > 0, me_y < count_y - 1

    loads = [
        pltpu.make_async_copy(source, target, load_sem.at[i])
        for i, (source, target) in enumerate([(lift_hbm, lift), (table_hbm, table)])
    ]
    for load in loads:
        load.start()

    def fetch(i, start, size):
        rows = pl.ds(start, size)
        return (
            pltpu.make_async_copy(rhs_hbm.at[rows], raw_r.at[rows], r_sem.at[i]),
            pltpu.make_async_copy(inv_hbm.at[rows], raw_b.at[rows], b_sem.at[i]),
        )

    whole = block // LANE
    depth = min(2, len(chunks))
    for i, (start, size) in list(enumerate(chunks))[:depth]:
        for copy in fetch(i, start, size):
            copy.start()

    barrier = pltpu.get_barrier_semaphore()
    for present, x, y in (
        (has_left, me_x - 1, me_y),
        (has_right, me_x + 1, me_y),
        (has_below, me_x, me_y - 1),
        (has_above, me_x, me_y + 1),
    ):
        @pl.when(present)
        def _():
            pl.semaphore_signal(barrier, inc=1, device_id=(x, y), device_id_type=MESH)

    part[...] = jnp.zeros_like(part)
    out[0] = jnp.zeros(out.shape[1:], out.dtype)

    @pl.when(me_x == 0)
    def _():
        inc[:, :, :LANE, :] = jnp.zeros((planes, CHUNKS, LANE, width), inc.dtype)

    @pl.when(me_y == 0)
    def _():
        inc[:, :, LANE:, :] = jnp.zeros((planes, CHUNKS, LANE, width), inc.dtype)

    row = lax.broadcasted_iota(jnp.int32, (3 * FACE, three), 0)
    col = lax.broadcasted_iota(jnp.int32, (3 * FACE, three), 1)
    face = jnp.where(col >= two, 2, jnp.where(col >= LANE, 1, 0))
    inside = col - face * LANE
    spread = ((inside < FACE) & (row == face * FACE + inside)).astype(jnp.float32).astype(jnp.bfloat16)
    loads[0].wait()
    padded[...] = lax.dot_general(
        lift[...], spread, (((0,), (0,)), ((), ())), preferred_element_type=jnp.float32
    ).astype(jnp.bfloat16)
    loads[1].wait()

    def split(raw, into, rows, size, lanes, t):
        mixed = raw[rows, :, lanes].astype(jnp.float32)
        wide_lanes = mixed.shape[-1]
        stage[t, : size * planes, :wide_lanes] = mixed.reshape(size * planes, wide_lanes)
        for s in range(planes):
            apart = stage[t, pl.ds(s, size, stride=planes), :]
            into[s, rows, lanes] = apart[:, :wide_lanes].astype(jnp.bfloat16)

    def arrange(i, start, size):
        for copy in fetch(i, start, size):
            copy.wait()
        if size == LANE:
            @pl.when(i + depth < whole)
            def _():
                for copy in fetch(i + depth, pl.multiple_of(start + depth * LANE, LANE), LANE):
                    copy.start()

            if whole < len(chunks):
                @pl.when(i + depth == whole)
                def _():
                    for copy in fetch(whole, *chunks[whole]):
                        copy.start()

        rows = pl.ds(start, size)
        for t, (first, wide_lanes) in enumerate(tiles):
            split(raw_b, inv, rows, size, slice(first, first + wide_lanes), t)
        for t in range(columns // LANE):
            split(raw_r, rhs, rows, size, slice(t * LANE, (t + 1) * LANE), len(tiles) + t)

    def arrange_full(i, carry):
        arrange(i, pl.multiple_of(i * LANE, LANE), LANE)
        return carry

    lax.fori_loop(0, whole, arrange_full, 0)
    for i, (start, size) in list(enumerate(chunks))[whole:]:
        arrange(i, start, size)

    def pick(source, put):
        for v in range(VARS):
            put(v * SQUARE, source[pl.ds(v * FACE + FACE - SQUARE, SQUARE), :])
        for v in range(VARS * NODES):
            put(LANE + v * NODES, source[pl.ds(v * SQUARE + SQUARE - NODES, NODES), :])
        put(two, source[pl.ds(NODES - 1, FACE, stride=NODES), :])

    def prepare(k):
        slot = order[k]
        for t, (first, wide_lanes) in enumerate(tiles):
            wide[t, :, :wide_lanes] = inv[slot, :, first : first + wide_lanes].astype(jnp.float32)

            def put(start, rows):
                part[t, pl.ds(start, rows.shape[0]), :] = rows

            pick(wide.at[t], put)
            picked[:, first : first + wide_lanes] = part[t, :, :wide_lanes].astype(jnp.bfloat16)
        moved = dot(picked[...], padded[...]).astype(jnp.bfloat16)
        for d in range(3):
            tile = slice(d * LANE, (d + 1) * LANE)
            trace_m[k, :, tile] = dot(moved[:, tile], table[orient[d, 0, slot]]).astype(jnp.bfloat16)
        plain = dot(picked[...], rhs[slot])
        for c in range(CHUNKS):
            trace_r[k, c] = plain[:, c * width : (c + 1) * width]

    def hop(k, c, axis):
        rows = pl.ds(axis * LANE, LANE)
        send, recv = ((x_send, x_recv), (y_send, y_recv))[axis]
        return pltpu.make_async_remote_copy(
            src_ref=out.at[k + 1, c, rows, :],
            dst_ref=inc.at[k, c, rows, :],
            send_sem=send.at[k, c],
            recv_sem=recv.at[k, c],
            device_id=((me_x + 1, me_y), (me_x, me_y + 1))[axis],
            device_id_type=MESH,
        )

    def advance(k, c):
        started = trace_r[k, c] - dot(trace_m[k, :, two:], out[k, c, two:, :])

        @pl.when(has_left)
        def _():
            hop(k, c, 0).wait_recv()

        @pl.when(has_below)
        def _():
            hop(k, c, 1).wait_recv()

        arrived = inc[k, c]
        ahead_rows = (started[:two] - dot(trace_m[k, :two, :two], arrived)).astype(jnp.bfloat16)
        out[k + 1, c, LANE:two, :] = ahead_rows[LANE:]

        @pl.when(has_above)
        def _():
            hop(k, c, 1).start()

        out[k + 1, c, :LANE, :] = ahead_rows[:LANE]

        @pl.when(has_right)
        def _():
            hop(k, c, 0).start()

        out[k + 1, c, two:, :] = (started[two:] - dot(trace_m[k, two:, :two], arrived)).astype(jnp.bfloat16)

    def finish(k):
        slot = order[k]
        faces = [[inc[k, c, d * LANE : (d + 1) * LANE, :] for c in range(CHUNKS)] for d in range(2)]
        faces.append([out[k, c, two:, :] for c in range(CHUNKS)])
        for d in range(3):
            face = jnp.concatenate(faces[d], axis=-1)
            turned[d * LANE : (d + 1) * LANE, :] = dot(table[orient[d, 0, slot]], face).astype(jnp.bfloat16)
        lifted = dot(padded[...], turned[...])
        source = (rhs[slot].astype(jnp.float32) - lifted).astype(jnp.bfloat16)
        sol[k] = dot(inv[slot], source).astype(jnp.bfloat16)

    distance = me_x + me_y
    lead = jnp.minimum(1 + 2 * distance, planes)
    near = distance * 2 <= count_x + count_y - 2

    def ahead(k, carry):
        prepare(k)
        return carry

    lax.fori_loop(0, lead, ahead, 0)

    neighbours = sum(p.astype(jnp.int32) for p in (has_left, has_right, has_below, has_above))
    pl.semaphore_wait(barrier, neighbours)

    def step(k, carry):
        for c in range(CHUNKS):
            advance(k, c)

        @pl.when(k + lead < planes)
        def _():
            prepare(k + lead)

        @pl.when(jnp.logical_not(near))
        def _():
            finish(k)

        return carry

    lax.fori_loop(0, planes, step, 0)

    @pl.when(near)
    def _():
        def late(k, carry):
            finish(k)
            return carry

        lax.fori_loop(0, planes, late, 0)

    def drain(k, carry):
        for c in range(CHUNKS):
            @pl.when(has_right)
            def _():
                hop(k, c, 0).wait_send()

            @pl.when(has_above)
            def _():
                hop(k, c, 1).wait_send()
        return carry

    lax.fori_loop(0, planes, drain, 0)


def place_kernel(order, sol, out, stage, ready, sems):
    planes, block, columns = sol.shape
    chunks = row_chunks(block)
    whole = block // LANE

    def put(i, start, size):
        rows = pl.ds(start, size)
        return pltpu.make_async_copy(ready.at[rows], out.at[rows], sems.at[i])

    def place(i, start, size):
        rows = pl.ds(start, size)
        for t in range(columns // LANE):
            lanes = slice(t * LANE, (t + 1) * LANE)
            for k in range(planes):
                stage[t, pl.ds(order[k], size, stride=planes), :] = sol[k, rows, lanes].astype(jnp.float32)
            ready[rows, :, lanes] = (
                stage[t, : size * planes, :].reshape(size, planes, LANE).astype(jnp.bfloat16)
            )
        put(i, start, size).start()

    def place_full(i, carry):
        place(i, pl.multiple_of(i * LANE, LANE), LANE)
        return carry

    lax.fori_loop(0, whole, place_full, 0)
    for i, (start, size) in list(enumerate(chunks))[whole:]:
        place(i, start, size)
    for i, (start, size) in enumerate(chunks):
        put(i, start, size).wait()


def on_device(right_side, inverse_blocks, lift_matrix, plane_order, face_orient):
    rhs = jnp.transpose(right_side, (0, 1, 3, 2, 4))[0, 0]
    inv = jnp.transpose(inverse_blocks, (0, 1, 3, 2, 4))[0, 0]
    order = plane_order[0, 0]
    orient = jnp.transpose(face_orient, (0, 3, 1, 2))[0]
    block, planes, columns = rhs.shape
    tiles = pl.cdiv(block, LANE)
    chunks = len(row_chunks(block))
    width = columns // CHUNKS
    two, three = 2 * LANE, 3 * LANE
    bf16, f32 = jnp.bfloat16, jnp.float32
    table = jnp.asarray(orient_table(), bf16)
    lift = lift_matrix.T
    smem = pl.BlockSpec(memory_space=pltpu.SMEM)
    vmem = pl.BlockSpec(memory_space=pltpu.VMEM)
    anywhere = pl.BlockSpec(memory_space=pl.ANY)
    sol = pl.pallas_call(
        sweep_kernel,
        out_shape=pltpu.VMEM((planes, block, columns), bf16),
        in_specs=[smem, smem] + [anywhere] * 4,
        out_specs=vmem,
        scratch_shapes=[
            pltpu.VMEM(table.shape, bf16),
            pltpu.VMEM(lift.shape, bf16),
            pltpu.VMEM(rhs.shape, bf16),
            pltpu.VMEM(inv.shape, bf16),
            pltpu.VMEM((tiles + columns // LANE, LANE * planes, LANE), f32),
            pltpu.VMEM((planes, block, columns), bf16),
            pltpu.VMEM((planes, block, block), bf16),
            pltpu.VMEM((block, three), bf16),
            pltpu.VMEM((three, columns), bf16),
            pltpu.VMEM((tiles, block, LANE), f32),
            pltpu.VMEM((tiles, three, LANE), f32),
            pltpu.VMEM((three, block), bf16),
            pltpu.VMEM((planes, three, three), bf16),
            pltpu.VMEM((planes, CHUNKS, three, width), f32),
            pltpu.VMEM((planes, CHUNKS, two, width), bf16),
            pltpu.VMEM((planes + 1, CHUNKS, three, width), bf16),
            pltpu.SemaphoreType.DMA((2,)),
            pltpu.SemaphoreType.DMA((chunks,)),
            pltpu.SemaphoreType.DMA((chunks,)),
            pltpu.SemaphoreType.DMA((planes, CHUNKS)),
            pltpu.SemaphoreType.DMA((planes, CHUNKS)),
            pltpu.SemaphoreType.DMA((planes, CHUNKS)),
            pltpu.SemaphoreType.DMA((planes, CHUNKS)),
        ],
        compiler_params=pltpu.CompilerParams(
            collective_id=0, has_side_effects=True, vmem_limit_bytes=60 * 1024 * 1024
        ),
    )(order, orient, table, lift, rhs, inv)
    result = pl.pallas_call(
        place_kernel,
        out_shape=jax.ShapeDtypeStruct(rhs.shape, bf16),
        in_specs=[smem, vmem],
        out_specs=anywhere,
        scratch_shapes=[
            pltpu.VMEM((columns // LANE, LANE * planes, LANE), f32),
            pltpu.VMEM(rhs.shape, bf16),
            pltpu.SemaphoreType.DMA((chunks,)),
        ],
        compiler_params=pltpu.CompilerParams(vmem_limit_bytes=16 * 1024 * 1024),
    )(order, sol)
    return jnp.transpose(result[None, None], (0, 1, 3, 2, 4))


def solution(mesh):
    placed = (
        P("gx", "gy", None, None, None),
        P("gx", "gy", None, None, None),
        P(),
        P("gx", "gy", None),
        P("gx", "gy", None, None),
    )
    return jax.shard_map(
        on_device,
        mesh=mesh,
        in_specs=placed,
        out_specs=P("gx", "gy", None, None, None),
        check_vma=False,
    )
```

```python
import functools

import jax
import jax.numpy as jnp
import numpy as np
from jax import lax
from jax.experimental import pallas as pl
from jax.experimental.pallas import tpu as pltpu
from jax.sharding import PartitionSpec as P

VARS = 5
NODES = 5
SQUARE = NODES * NODES
FACE = VARS * SQUARE
BLOCK = FACE * NODES
LANE = 128
CHUNKS = 1
MESH = pl.DeviceIdType.MESH


def orient_table():
    table = np.zeros((8, LANE, LANE), np.float32)
    for orient in range(8):
        for variable in range(VARS):
            for first in range(NODES):
                for second in range(NODES):
                    p, q = (second, first) if orient & 1 else (first, second)
                    if orient & 2:
                        p = NODES - 1 - p
                    if orient & 4:
                        q = NODES - 1 - q
                    target = variable * SQUARE + first * NODES + second
                    table[orient, target, variable * SQUARE + p * NODES + q] = 1.0
    return table


def dot(a, b):
    return jnp.dot(a, b, preferred_element_type=jnp.float32)


def row_chunks(block):
    return [(start, min(LANE, block - start)) for start in range(0, block, LANE)]


def sweep_kernel(
    order, orient, table_hbm, lift_hbm, rhs_hbm, inv_hbm, sol,
    table, lift, raw_r, raw_b, stage, rhs, inv, padded, turned, wide, part, picked, trace_m, trace_r,
    inc, out, load_sem, r_sem, b_sem, x_send, y_send, x_recv, y_recv,
):
    planes, block, columns = rhs.shape
    width = columns // CHUNKS
    two, three = 2 * LANE, 3 * LANE
    chunks = row_chunks(block)
    tiles = [(t, min(LANE, block - t)) for t in range(0, block, LANE)]
    count_x, count_y = lax.axis_size("gx"), lax.axis_size("gy")
    me_x, me_y = lax.axis_index("gx"), lax.axis_index("gy")
    has_left, has_right = me_x > 0, me_x < count_x - 1
    has_below, has_above = me_y > 0, me_y < count_y - 1

    loads = [
        pltpu.make_async_copy(source, target, load_sem.at[i])
        for i, (source, target) in enumerate([(lift_hbm, lift), (table_hbm, table)])
    ]
    for load in loads:
        load.start()

    def fetch(i, start, size):
        rows = pl.ds(start, size)
        return (
            pltpu.make_async_copy(rhs_hbm.at[rows], raw_r.at[rows], r_sem.at[i]),
            pltpu.make_async_copy(inv_hbm.at[rows], raw_b.at[rows], b_sem.at[i]),
        )

    whole = block // LANE
    depth = min(2, len(chunks))
    for i, (start, size) in list(enumerate(chunks))[:depth]:
        for copy in fetch(i, start, size):
            copy.start()

    barrier = pltpu.get_barrier_semaphore()
    for present, x, y in (
        (has_left, me_x - 1, me_y),
        (has_right, me_x + 1, me_y),
        (has_below, me_x, me_y - 1),
        (has_above, me_x, me_y + 1),
    ):
        @pl.when(present)
        def _():
            pl.semaphore_signal(barrier, inc=1, device_id=(x, y), device_id_type=MESH)

    part[...] = jnp.zeros_like(part)
    out[0] = jnp.zeros(out.shape[1:], out.dtype)

    @pl.when(me_x == 0)
    def _():
        inc[:, :, :LANE, :] = jnp.zeros((planes, CHUNKS, LANE, width), inc.dtype)

    @pl.when(me_y == 0)
    def _():
        inc[:, :, LANE:, :] = jnp.zeros((planes, CHUNKS, LANE, width), inc.dtype)

    row = lax.broadcasted_iota(jnp.int32, (3 * FACE, three), 0)
    col = lax.broadcasted_iota(jnp.int32, (3 * FACE, three), 1)
    face = jnp.where(col >= two, 2, jnp.where(col >= LANE, 1, 0))
    inside = col - face * LANE
    spread = ((inside < FACE) & (row == face * FACE + inside)).astype(jnp.float32).astype(jnp.bfloat16)
    loads[0].wait()
    padded[...] = lax.dot_general(
        lift[...], spread, (((0,), (0,)), ((), ())), preferred_element_type=jnp.float32
    ).astype(jnp.bfloat16)
    loads[1].wait()

    def split(raw, into, rows, size, lanes, t):
        mixed = raw[rows, :, lanes].astype(jnp.float32)
        wide_lanes = mixed.shape[-1]
        stage[t, : size * planes, :wide_lanes] = mixed.reshape(size * planes, wide_lanes)
        for s in range(planes):
            apart = stage[t, pl.ds(s, size, stride=planes), :]
            into[s, rows, lanes] = apart[:, :wide_lanes].astype(jnp.bfloat16)

    def arrange(i, start, size):
        for copy in fetch(i, start, size):
            copy.wait()
        if size == LANE:
            @pl.when(i + depth < whole)
            def _():
                for copy in fetch(i + depth, pl.multiple_of(start + depth * LANE, LANE), LANE):
                    copy.start()

            if whole < len(chunks):
                @pl.when(i + depth == whole)
                def _():
                    for copy in fetch(whole, *chunks[whole]):
                        copy.start()

        rows = pl.ds(start, size)
        for t, (first, wide_lanes) in enumerate(tiles):
            split(raw_b, inv, rows, size, slice(first, first + wide_lanes), t)
        for t in range(columns // LANE):
            split(raw_r, rhs, rows, size, slice(t * LANE, (t + 1) * LANE), len(tiles) + t)

    def arrange_full(i, carry):
        arrange(i, pl.multiple_of(i * LANE, LANE), LANE)
        return carry

    lax.fori_loop(0, whole, arrange_full, 0)
    for i, (start, size) in list(enumerate(chunks))[whole:]:
        arrange(i, start, size)

    def pick(source, put):
        for v in range(VARS):
            put(v * SQUARE, source[pl.ds(v * FACE + FACE - SQUARE, SQUARE), :])
        for v in range(VARS * NODES):
            put(LANE + v * NODES, source[pl.ds(v * SQUARE + SQUARE - NODES, NODES), :])
        put(two, source[pl.ds(NODES - 1, FACE, stride=NODES), :])

    def prepare(k):
        slot = order[k]
        for t, (first, wide_lanes) in enumerate(tiles):
            wide[t, :, :wide_lanes] = inv[slot, :, first : first + wide_lanes].astype(jnp.float32)

            def put(start, rows):
                part[t, pl.ds(start, rows.shape[0]), :] = rows

            pick(wide.at[t], put)
            picked[:, first : first + wide_lanes] = part[t, :, :wide_lanes].astype(jnp.bfloat16)
        moved = dot(picked[...], padded[...]).astype(jnp.bfloat16)
        for d in range(3):
            tile = slice(d * LANE, (d + 1) * LANE)
            trace_m[k, :, tile] = dot(moved[:, tile], table[orient[d, 0, slot]]).astype(jnp.bfloat16)
        plain = dot(picked[...], rhs[slot])
        for c in range(CHUNKS):
            trace_r[k, c] = plain[:, c * width : (c + 1) * width]

    def hop(k, c, axis):
        rows = pl.ds(axis * LANE, LANE)
        send, recv = ((x_send, x_recv), (y_send, y_recv))[axis]
        return pltpu.make_async_remote_copy(
            src_ref=out.at[k + 1, c, rows, :],
            dst_ref=inc.at[k, c, rows, :],
            send_sem=send.at[k, c],
            recv_sem=recv.at[k, c],
            device_id=((me_x + 1, me_y), (me_x, me_y + 1))[axis],
            device_id_type=MESH,
        )

    def advance(k, c):
        started = trace_r[k, c] - dot(trace_m[k, :, two:], out[k, c, two:, :])

        @pl.when(has_left)
        def _():
            hop(k, c, 0).wait_recv()

        @pl.when(has_below)
        def _():
            hop(k, c, 1).wait_recv()

        arrived = inc[k, c]
        ahead_rows = (started[:two] - dot(trace_m[k, :two, :two], arrived)).astype(jnp.bfloat16)
        out[k + 1, c, LANE:two, :] = ahead_rows[LANE:]

        @pl.when(has_above)
        def _():
            hop(k, c, 1).start()

        out[k + 1, c, :LANE, :] = ahead_rows[:LANE]

        @pl.when(has_right)
        def _():
            hop(k, c, 0).start()

        out[k + 1, c, two:, :] = (started[two:] - dot(trace_m[k, two:, :two], arrived)).astype(jnp.bfloat16)

    def finish(k):
        slot = order[k]
        faces = [[inc[k, c, d * LANE : (d + 1) * LANE, :] for c in range(CHUNKS)] for d in range(2)]
        faces.append([out[k, c, two:, :] for c in range(CHUNKS)])
        for d in range(3):
            face = jnp.concatenate(faces[d], axis=-1)
            turned[d * LANE : (d + 1) * LANE, :] = dot(table[orient[d, 0, slot]], face).astype(jnp.bfloat16)
        lifted = dot(padded[...], turned[...])
        source = (rhs[slot].astype(jnp.float32) - lifted).astype(jnp.bfloat16)
        sol[k] = dot(inv[slot], source).astype(jnp.bfloat16)

    distance = me_x + me_y
    lead = jnp.minimum(1 + 2 * distance, planes)
    near = distance * 2 <= count_x + count_y - 2

    def ahead(k, carry):
        prepare(k)
        return carry

    lax.fori_loop(0, lead, ahead, 0)

    neighbours = sum(p.astype(jnp.int32) for p in (has_left, has_right, has_below, has_above))
    pl.semaphore_wait(barrier, neighbours)

    def step(k, carry):
        for c in range(CHUNKS):
            advance(k, c)

        @pl.when(k + lead < planes)
        def _():
            prepare(k + lead)

        @pl.when(jnp.logical_not(near))
        def _():
            finish(k)

        return carry

    lax.fori_loop(0, planes, step, 0)

    @pl.when(near)
    def _():
        def late(k, carry):
            finish(k)
            return carry

        lax.fori_loop(0, planes, late, 0)

    def drain(k, carry):
        for c in range(CHUNKS):
            @pl.when(has_right)
            def _():
                hop(k, c, 0).wait_send()

            @pl.when(has_above)
            def _():
                hop(k, c, 1).wait_send()
        return carry

    lax.fori_loop(0, planes, drain, 0)


def place_kernel(order, sol, out, stage, ready, sems):
    planes, block, columns = sol.shape
    chunks = row_chunks(block)
    whole = block // LANE

    def put(i, start, size):
        rows = pl.ds(start, size)
        return pltpu.make_async_copy(ready.at[rows], out.at[rows], sems.at[i])

    def place(i, start, size):
        rows = pl.ds(start, size)
        for t in range(columns // LANE):
            lanes = slice(t * LANE, (t + 1) * LANE)
            for k in range(planes):
                stage[t, pl.ds(order[k], size, stride=planes), :] = sol[k, rows, lanes].astype(jnp.float32)
            ready[rows, :, lanes] = (
                stage[t, : size * planes, :].reshape(size, planes, LANE).astype(jnp.bfloat16)
            )
        put(i, start, size).start()

    def place_full(i, carry):
        place(i, pl.multiple_of(i * LANE, LANE), LANE)
        return carry

    lax.fori_loop(0, whole, place_full, 0)
    for i, (start, size) in list(enumerate(chunks))[whole:]:
        place(i, start, size)
    for i, (start, size) in enumerate(chunks):
        put(i, start, size).wait()


def on_device(right_side, inverse_blocks, lift_matrix, plane_order, face_orient):
    rhs = jnp.transpose(right_side, (0, 1, 3, 2, 4))[0, 0]
    inv = jnp.transpose(inverse_blocks, (0, 1, 3, 2, 4))[0, 0]
    order = plane_order[0, 0]
    orient = jnp.transpose(face_orient, (0, 3, 1, 2))[0]
    block, planes, columns = rhs.shape
    tiles = pl.cdiv(block, LANE)
    chunks = len(row_chunks(block))
    width = columns // CHUNKS
    two, three = 2 * LANE, 3 * LANE
    bf16, f32 = jnp.bfloat16, jnp.float32
    table = jnp.asarray(orient_table(), bf16)
    lift = lift_matrix.T
    smem = pl.BlockSpec(memory_space=pltpu.SMEM)
    vmem = pl.BlockSpec(memory_space=pltpu.VMEM)
    anywhere = pl.BlockSpec(memory_space=pl.ANY)
    sol = pl.pallas_call(
        sweep_kernel,
        out_shape=pltpu.VMEM((planes, block, columns), bf16),
        in_specs=[smem, smem] + [anywhere] * 4,
        out_specs=vmem,
        scratch_shapes=[
            pltpu.VMEM(table.shape, bf16),
            pltpu.VMEM(lift.shape, bf16),
            pltpu.VMEM(rhs.shape, bf16),
            pltpu.VMEM(inv.shape, bf16),
            pltpu.VMEM((tiles + columns // LANE, LANE * planes, LANE), f32),
            pltpu.VMEM((planes, block, columns), bf16),
            pltpu.VMEM((planes, block, block), bf16),
            pltpu.VMEM((block, three), bf16),
            pltpu.VMEM((three, columns), bf16),
            pltpu.VMEM((tiles, block, LANE), f32),
            pltpu.VMEM((tiles, three, LANE), f32),
            pltpu.VMEM((three, block), bf16),
            pltpu.VMEM((planes, three, three), bf16),
            pltpu.VMEM((planes, CHUNKS, three, width), f32),
            pltpu.VMEM((planes, CHUNKS, two, width), bf16),
            pltpu.VMEM((planes + 1, CHUNKS, three, width), bf16),
            pltpu.SemaphoreType.DMA((2,)),
            pltpu.SemaphoreType.DMA((chunks,)),
            pltpu.SemaphoreType.DMA((chunks,)),
            pltpu.SemaphoreType.DMA((planes, CHUNKS)),
            pltpu.SemaphoreType.DMA((planes, CHUNKS)),
            pltpu.SemaphoreType.DMA((planes, CHUNKS)),
            pltpu.SemaphoreType.DMA((planes, CHUNKS)),
        ],
        compiler_params=pltpu.CompilerParams(
            collective_id=0, has_side_effects=True, vmem_limit_bytes=60 * 1024 * 1024
        ),
    )(order, orient, table, lift, rhs, inv)
    result = pl.pallas_call(
        place_kernel,
        out_shape=jax.ShapeDtypeStruct(rhs.shape, bf16),
        in_specs=[smem, vmem],
        out_specs=anywhere,
        scratch_shapes=[
            pltpu.VMEM((columns // LANE, LANE * planes, LANE), f32),
            pltpu.VMEM(rhs.shape, bf16),
            pltpu.SemaphoreType.DMA((chunks,)),
        ],
        compiler_params=pltpu.CompilerParams(vmem_limit_bytes=16 * 1024 * 1024),
    )(order, sol)
    return jnp.transpose(result[None, None], (0, 1, 3, 2, 4))


def solution(mesh):
    placed = (
        P("gx", "gy", None, None, None),
        P("gx", "gy", None, None, None),
        P(),
        P("gx", "gy", None),
        P("gx", "gy", None, None),
    )
    return jax.shard_map(
        on_device,
        mesh=mesh,
        in_specs=placed,
        out_specs=P("gx", "gy", None, None, None),
        check_vma=False,
    )
```
